256 devices in a mesh: seq: 32 (over x, z), head: 8 (over y, core).
Axes of the slice: x: 4, y: 4, z: 8, core: 2. Of those that a mesh axis runs over, the one named last changes fastest.
Arguments:
- queries: bfloat16 [32768, 5120], P('seq', 'head')
- keys: bfloat16 [32768, 5120], P('seq', 'head')
- values: bfloat16 [32768, 5120], P('seq', 'head'), may hold values from -6 to 6
- query_gain: float32 [5120], P('head'), may hold values from 0.1 to 1.9
- key_gain: float32 [5120], P('head'), may hold values from 0.1 to 1.9
- shapes: int32 [8, 3], replicated, may hold values from 4 to 32, as said below
- windows: int32 [256, 27], P('seq'), may hold values from -1 to 255, as said below
- text_keys: bfloat16 [32, 256, 5120], P(None, 'seq', 'head')
- text_values: bfloat16 [32, 256, 5120], P(None, 'seq', 'head'), may hold values from -6 to 6
- owner: int32 [8], replicated, may hold values from 0 to 31, as said below
Outputs:
- attended: bfloat16 [32768, 5120], P('seq', 'head')
The draws below stay inside these ranges and needn't reach their ends.
Inputs may be any that keep to these rules, and one draw needn't show every extreme that they name: `shapes`: row s is (frames, height, width) of video s in tokens: height and width are 16 and 32, or 32 and 16, so a frame has 4 tiles; each video has from 16 to 48 tiles, and the videos' tiles add up to 256, so no tile holds tokens of two videos. `windows`: entry k of row g stands for the tile k // 9 - 1 frames, (k // 3) % 3 - 1 tile rows and k % 3 - 1 tile columns away from tile g in its video: it holds that tile's number or -1; it is -1 wherever that tile lies outside the video, and entry 13 is always g. `owner`: no two videos share a panel.
All inputs are finite; a program needn't handle non-finite values.
Results may differ from the reference program's by a relative error of at most 0.012.
Values may be sent and summed in bfloat16 or wider, within the bound.
A program may use at most 128 MiB of HBM per device.

```python
import jax
import jax.numpy as jnp
from jax import lax

HEAD_DIM = 128
HEADS = 40
D = 5120
TILE_H = 8
TILE_W = 16
TILE = 128
WIN = 27
REACH = 7
TXT = 256
TILES_DEV = 8
TOKENS = 32768
NTILES = 256
SAMPLES = 8
PANELS = 32


def sample_shapes(key):
    half_count = SAMPLES // 2
    units = jax.random.randint(jax.random.fold_in(key, 11), (half_count,), TILES_DEV // 2, 3 * TILES_DEV // 2 + 1)
    units = units.at[0].set(3 * TILES_DEV // 2)
    partner = jax.random.permutation(jax.random.fold_in(key, 12), half_count)
    tile_counts = 4 * jnp.concatenate([units, 2 * TILES_DEV - units[partner]])
    shuffle = jax.random.permutation(jax.random.fold_in(key, 13), SAMPLES)
    tile_counts = tile_counts[shuffle]
    landscape = jax.random.randint(jax.random.fold_in(key, 14), (SAMPLES,), 0, 2) == 1
    landscape = jnp.where(tile_counts == 6 * TILES_DEV, True, jnp.where(tile_counts == 2 * TILES_DEV, False, landscape))
    row_counts = jnp.where(landscape, 2, 4)
    col_counts = jnp.where(landscape, 2, 1)
    frame_counts = tile_counts // 4
    return jnp.stack([frame_counts, row_counts * TILE_H, col_counts * TILE_W], axis=1).astype(jnp.int32)


def draw_shapes(key, part):
    return sample_shapes(key)


def draw_windows(key, part):
    shape_rows = sample_shapes(key)
    row_counts = shape_rows[:, 1] // TILE_H
    col_counts = shape_rows[:, 2] // TILE_W
    tile_counts = shape_rows[:, 0] * row_counts * col_counts
    tile_ends = jnp.cumsum(tile_counts).astype(jnp.int32)
    tile_starts = tile_ends - tile_counts
    tile_ids = jnp.arange(NTILES, dtype=jnp.int32)
    sample_ids = jnp.sum((tile_ids[:, None] >= tile_ends[None, :]).astype(jnp.int32), axis=1)
    first_tiles = tile_starts[sample_ids]
    rows_here = row_counts[sample_ids]
    cols_here = col_counts[sample_ids]
    frame_counts = shape_rows[sample_ids, 0]
    offsets = tile_ids - first_tiles
    per_frame = rows_here * cols_here
    frames = offsets // per_frame
    within = offsets % per_frame
    bands = within // cols_here
    columns = within % cols_here
    slots = jnp.arange(WIN, dtype=jnp.int32)
    time_step = slots // 9 - 1
    band_step = slots // 3 % 3 - 1
    column_step = slots % 3 - 1
    near_frame = frames[:, None] + time_step[None, :]
    near_band = bands[:, None] + band_step[None, :]
    near_column = columns[:, None] + column_step[None, :]
    inside = (near_frame >= 0) & (near_frame < frame_counts[:, None]) & (near_band >= 0) & (near_band < rows_here[:, None]) & (near_column >= 0) & (near_column < cols_here[:, None])
    chosen = jax.random.randint(jax.random.fold_in(key, 21), (NTILES, WIN), 0, 2) == 1
    chosen = chosen | ((time_step == 0) & (band_step == 0) & (column_step == 0))[None, :]
    near_ids = first_tiles[:, None] + near_frame * per_frame[:, None] + near_band * cols_here[:, None] + near_column
    return jnp.where(inside & chosen, near_ids, -1).astype(jnp.int32)


def feature_field(key):
    columns = jnp.arange(D, dtype=jnp.float32) / D
    rough = jnp.exp(jax.random.uniform(jax.random.fold_in(key, 31), (D,), minval=-0.35, maxval=0.35))
    column_scale = 3.0 ** (0.5 * columns) * rough
    row_scale = jnp.exp(jax.random.uniform(jax.random.fold_in(key, 32), (TOKENS, 1), minval=0.0, maxval=2.31))
    entries = jax.random.normal(jax.random.fold_in(key, 33), (TOKENS, D), dtype=jnp.float32)
    return entries * row_scale * column_scale[None, :]


def draw_queries(key, part):
    return feature_field(jax.random.fold_in(key, 41)).astype(jnp.bfloat16)


def draw_keys(key, part):
    return feature_field(jax.random.fold_in(key, 42)).astype(jnp.bfloat16)


def draw_text_keys(key, part):
    inner_key = jax.random.fold_in(key, 51)
    entries = jax.random.normal(inner_key, (PANELS, TXT, D), dtype=jnp.float32)
    return entries.astype(jnp.bfloat16)


def draw_owner(key, part):
    others = jax.random.permutation(jax.random.fold_in(key, 61), PANELS - 1)[:SAMPLES - 1].astype(jnp.int32)
    chosen = jnp.concatenate([others, jnp.full((1,), PANELS - 1, dtype=jnp.int32)])
    order = jax.random.permutation(jax.random.fold_in(key, 62), SAMPLES)
    return chosen[order].astype(jnp.int32)


def level_of(own_key, shape, pieces, least, high):
    level, own = 1.0, jax.random.fold_in(own_key, 6)
    for axis_at, shards_of in pieces:
        steps = jnp.exp(jax.random.uniform(jax.random.fold_in(own, axis_at), (shards_of,), jnp.float32, least / len(pieces), high / len(pieces)))
        level = level * jnp.repeat(steps, shape[axis_at] // shards_of).reshape([-1 if axis == axis_at else 1 for axis in range(len(shape))])
    return level


def noise(key, dims, deviation, reach, pieces=(), kind=jnp.bfloat16):
    drawn = deviation * jax.random.normal(key, dims, jnp.float32)
    if pieces:
        drawn = drawn * level_of(key, dims, pieces, -0.22, 0.18)
    return jnp.clip(drawn, -reach, reach).astype(kind)


def setup_inputs(seed: int = 0) -> dict:
    splits = jax.random.split(jax.random.key(seed), 11)
    return {
        "queries": draw_queries(jax.random.fold_in(splits[10], 71), 0),
        "keys": draw_keys(jax.random.fold_in(splits[10], 71), 0),
        "values": noise(splits[2], (TOKENS, D), 1.0, 6.0, ((0, 32), (1, 8))),
        "query_gain": jnp.clip(1.0 + 0.18 * jax.random.normal(splits[3], (D,), jnp.float32), 0.1, 1.9),
        "key_gain": jnp.clip(1.0 + 0.18 * jax.random.normal(splits[4], (D,), jnp.float32), 0.1, 1.9),
        "shapes": draw_shapes(jax.random.fold_in(splits[10], 71), 0),
        "windows": draw_windows(jax.random.fold_in(splits[10], 71), 0),
        "text_keys": draw_text_keys(jax.random.fold_in(splits[10], 71), 0),
        "text_values": noise(splits[8], (PANELS, TXT, D), 1.0, 6.0, ((1, 32), (2, 8))),
        "owner": draw_owner(jax.random.fold_in(splits[10], 71), 0),
    }


epsilon = 1e-06

def tile_table(shape_rows):
    per_frame = shape_rows[:, 1] // TILE_H * (shape_rows[:, 2] // TILE_W)
    tile_counts = shape_rows[:, 0] * per_frame
    tile_ends = jnp.cumsum(tile_counts).astype(jnp.int32)
    return ((tile_ends - tile_counts).astype(jnp.int32), tile_ends)

def locate(tile_ids, shape_rows, tile_starts, tile_ends):
    sample_ids = lax.optimization_barrier(jnp.sum((tile_ids[:, None] >= tile_ends[None, :]).astype(jnp.int32), axis=1)).astype(jnp.int32)
    one_hot = (sample_ids[:, None] == jnp.arange(tile_ends.shape[0], dtype=jnp.int32)[None, :]).astype(jnp.int32)
    first_tiles = lax.optimization_barrier(jnp.sum(one_hot * tile_starts[None, :], axis=1)).astype(jnp.int32)
    row_counts = lax.optimization_barrier(jnp.sum(one_hot * (shape_rows[:, 1] // TILE_H)[None, :], axis=1)).astype(jnp.int32)
    col_counts = lax.optimization_barrier(jnp.sum(one_hot * (shape_rows[:, 2] // TILE_W)[None, :], axis=1)).astype(jnp.int32)
    offsets = tile_ids - first_tiles
    per_frame = row_counts * col_counts
    within = offsets % per_frame
    return (sample_ids, one_hot, offsets // per_frame, within // col_counts, within % col_counts)

def rope_angles(frames, bands, columns, head_size):
    inner = jnp.arange(TILE_H * TILE_W, dtype=jnp.int32)
    tile_total = frames.shape[0]
    time_pos = jnp.broadcast_to(frames[:, None], (tile_total, inner.shape[0])).reshape(-1).astype(jnp.float32)
    row_pos = (bands[:, None] * TILE_H + inner[None, :] // TILE_W).reshape(-1).astype(jnp.float32)
    col_pos = (columns[:, None] * TILE_W + inner[None, :] % TILE_W).reshape(-1).astype(jnp.float32)
    third = head_size // 6
    part_sizes = (head_size - 4 * third, 2 * third, 2 * third)
    angle_parts = []
    for position, part_size in zip((time_pos, row_pos, col_pos), part_sizes):
        frequency = 10000.0 ** (-jnp.arange(0, part_size, 2, dtype=jnp.float32) / part_size)
        angle_parts.append(position[:, None] * frequency[None, :])
    return jnp.concatenate(angle_parts, axis=1)

def rotate(field, angles):
    paired = field.reshape(field.shape[0], field.shape[1], field.shape[2] // 2, 2)
    cosine = jnp.cos(angles)[:, None, :]
    sine = jnp.sin(angles)[:, None, :]
    even_part = paired[..., 0]
    odd_part = paired[..., 1]
    turned = jnp.stack([even_part * cosine - odd_part * sine, even_part * sine + odd_part * cosine], axis=-1)
    return turned.reshape(field.shape)

def reference(queries, keys, values, query_gain, key_gain, shapes, windows, text_keys, text_values, owner):
    tile_starts, tile_ends = tile_table(shapes)
    tile_ids = jnp.arange(NTILES, dtype=jnp.int32)
    sample_ids, one_hot, frames, bands, columns = locate(tile_ids, shapes, tile_starts, tile_ends)
    panel_ids = lax.optimization_barrier(jnp.sum(one_hot * owner[None, :], axis=1)).astype(jnp.int32)

    def make_prepare(gain):

        def prepare(items):
            block_rows, frame_one, band_one, column_one = items
            angles = rope_angles(frame_one[None], band_one[None], column_one[None], HEAD_DIM)
            widened = block_rows.astype(jnp.float32)
            scaled = widened * lax.rsqrt(lax.optimization_barrier(jnp.mean(widened * widened, axis=1, keepdims=True)) + epsilon) * gain[None, :]
            return rotate(scaled.reshape(TILE, HEADS, HEAD_DIM), angles).astype(jnp.bfloat16)
        return prepare
    q_hat = lax.map(make_prepare(query_gain), (queries.reshape(NTILES, TILE, D), frames, bands, columns)).reshape(TOKENS, HEADS, HEAD_DIM)
    k_hat = lax.map(make_prepare(key_gain), (keys.reshape(NTILES, TILE, D), frames, bands, columns)).reshape(TOKENS, HEADS, HEAD_DIM)
    margin = REACH * TILE
    k_padded = jnp.pad(k_hat, ((margin, margin), (0, 0), (0, 0)))
    v_padded = jnp.pad(values.reshape(TOKENS, HEADS, HEAD_DIM), ((margin, margin), (0, 0), (0, 0)))
    span_rows = (2 * REACH + 1) * TILE
    factor = HEAD_DIM ** (-0.5)

    def attend(tile_index):
        query_rows = lax.dynamic_slice_in_dim(q_hat, tile_index * TILE, TILE, 0).astype(jnp.float32)
        key_rows = lax.dynamic_slice_in_dim(k_padded, tile_index * TILE, span_rows, 0)
        value_rows = lax.dynamic_slice_in_dim(v_padded, tile_index * TILE, span_rows, 0)
        panel = lax.dynamic_index_in_dim(panel_ids, tile_index, 0, keepdims=False)
        prompt_keys = lax.dynamic_index_in_dim(text_keys, panel, 0, keepdims=False).reshape(TXT, HEADS, HEAD_DIM)
        prompt_values = lax.dynamic_index_in_dim(text_values, panel, 0, keepdims=False).reshape(TXT, HEADS, HEAD_DIM)
        key_tiles = tile_index - REACH + jnp.arange(2 * REACH + 1, dtype=jnp.int32)
        listed = lax.dynamic_index_in_dim(windows, tile_index, 0, keepdims=False)
        allowed = jnp.any(listed[:, None] == key_tiles[None, :], axis=0) & (key_tiles >= 0)
        key_mask = jnp.concatenate([jnp.repeat(allowed, TILE), jnp.ones((TXT,), dtype=bool)])
        all_keys = jnp.concatenate([key_rows, prompt_keys], axis=0).astype(jnp.float32)
        all_values = jnp.concatenate([value_rows, prompt_values], axis=0).astype(jnp.float32)
        scores = jnp.einsum('qhd,khd->hqk', query_rows, all_keys) * factor
        scores = jnp.where(key_mask[None, None, :], scores, -jnp.inf)
        largest = lax.optimization_barrier(jnp.max(scores, axis=-1, keepdims=True))
        weights = jnp.exp(scores - largest)
        totals = lax.optimization_barrier(jnp.sum(weights, axis=-1))
        rounded = lax.optimization_barrier(weights.astype(jnp.bfloat16))
        mixed = jnp.einsum('hqk,khd->qhd', rounded.astype(jnp.float32), all_values)
        mixed = mixed / jnp.transpose(totals)[:, :, None]
        return mixed.astype(jnp.bfloat16).reshape(TILE, D)
    return lax.map(attend, tile_ids).reshape(TOKENS, D)
```

```python
import jax
import jax.numpy as jnp
import numpy as np
from jax import lax
from jax.experimental import pallas as pl
from jax.experimental.pallas import tpu as pltpu
from jax.sharding import PartitionSpec as P

MESH = pl.DeviceIdType.MESH
HEAD_DIM = 128
D = 5120
TILE = 128
FRAME = 512
ROWS = 1024
HEADS = 5
TXT = 256
PANELS = 32
SAMPLES = 8
SEQ = 32
HEAD = 8
TXT_ROWS = 8
EPSILON = 1e-06
MASKED = -1e30
TIMES = 16


def rope_tables():
    third = HEAD_DIM // 6
    sizes = (HEAD_DIM - 4 * third, 2 * third, 2 * third)
    lane = np.arange(HEAD_DIM)
    parts = []
    start = 0
    for size, count in zip(sizes, (TIMES, 32, 32)):
        frequency = (np.float32(10000.0) ** (-np.arange(0, size, 2, dtype=np.float32) / np.float32(size))).astype(np.float32)
        angle = np.arange(count, dtype=np.float32)[:, None] * frequency[None, :]
        cosine = np.zeros((count, HEAD_DIM), np.float32)
        sine = np.zeros((count, HEAD_DIM), np.float32)
        cosine[:, start : start + size] = np.repeat(np.cos(angle), 2, axis=1)
        sine[:, start : start + size] = np.repeat(np.sin(angle), 2, axis=1)
        even = lane % 2 == 0
        parts.append(np.stack([cosine, np.where(even, -sine, 0.0), np.where(even, 0.0, sine)]).astype(np.float32))
        start += size
    time, row, col = parts
    return time, row.reshape(3, 4, 8, HEAD_DIM), col.reshape(3, 2, 16, HEAD_DIM)


def kernel(
    shapes, windows, owner, query_gain, key_gain, time_tab, row_tab, col_tab,
    q_hbm, k_hbm, v_hbm, tk_hbm, tv_hbm, out_hbm,
    qx, kx, vx, text, send, got, hk, hv, squares, peer_squares, totals, halo_totals,
    inverse, cos_h, sina_h, sinb_h, inv_h, outs, bias,
    load_sem, halo_send, halo_recv, sq_send, sq_recv, tot_send, tot_recv, txt_send, txt_recv, own_sem, out_sem,
):
    seq = lax.axis_index("seq")
    head = lax.axis_index("head")
    right = lax.rem(seq + 1, SEQ)
    left = lax.rem(seq + SEQ - 1, SEQ)

    loads = []
    for h in range(HEADS):
        lanes = pl.ds(h * HEAD_DIM, HEAD_DIM)
        loads.append(pltpu.make_async_copy(k_hbm.at[:, lanes], kx.at[h], load_sem.at[0, h]))
        loads.append(pltpu.make_async_copy(q_hbm.at[:, lanes], qx.at[h], load_sem.at[1, h]))
        loads.append(pltpu.make_async_copy(v_hbm.at[:, lanes], vx.at[h], load_sem.at[2, h]))
    loads.append(pltpu.make_async_copy(tk_hbm, text.at[0], load_sem.at[0, HEADS]))
    loads.append(pltpu.make_async_copy(tv_hbm, text.at[1], load_sem.at[1, HEADS]))
    for load in loads:
        load.start()

    barrier = pltpu.get_barrier_semaphore()

    def greet_seq(j, carry):
        pl.semaphore_signal(barrier, inc=1, device_id={"seq": lax.rem(seq + j, SEQ), "head": head}, device_id_type=MESH)
        return carry

    def greet_head(j, carry):
        pl.semaphore_signal(barrier, inc=1, device_id={"seq": seq, "head": lax.rem(head + j, HEAD)}, device_id_type=MESH)
        return carry

    lax.fori_loop(1, SEQ, greet_seq, 0)
    lax.fori_loop(1, HEAD, greet_head, 0)
    for load in loads:
        load.wait()

    def square_tile(i, carry):
        at = pl.ds(pl.multiple_of(i * TILE, TILE), TILE)
        for base, x in ((0, qx), (8, kx)):
            total = jnp.zeros((TILE, HEAD_DIM), jnp.float32)
            for h in range(HEADS):
                wide = x[h, at, :].astype(jnp.float32)
                total = total + wide * wide
            squares[pl.ds(base + i, 1), :] = jnp.sum(total.T, axis=0, keepdims=True)
        return carry

    lax.fori_loop(0, 8, square_tile, 0)
    pl.semaphore_wait(barrier, SEQ - 1 + HEAD - 1)

    def halo_copy(h, kv, direction):
        source = (k_hbm, v_hbm)[kv]
        target = (hk, hv)[kv]
        lanes = pl.ds(pl.multiple_of(h * HEAD_DIM, HEAD_DIM), HEAD_DIM)
        return pltpu.make_async_remote_copy(
            src_ref=source.at[pl.ds((1 - direction) * FRAME, FRAME), lanes],
            dst_ref=target.at[direction, h],
            send_sem=halo_send.at[direction, kv, h],
            recv_sem=halo_recv.at[direction, kv, h],
            device_id={"seq": (right, left)[direction], "head": head},
            device_id_type=MESH,
        )

    def halo_start(h, carry):
        for kv in range(2):
            for direction in range(2):
                halo_copy(h, kv, direction).start()
        return carry

    def square_copy(j):
        return pltpu.make_async_remote_copy(
            src_ref=squares,
            dst_ref=peer_squares.at[j - 1],
            send_sem=sq_send.at[j - 1],
            recv_sem=sq_recv.at[j - 1],
            device_id={"seq": seq, "head": lax.rem(head + j, HEAD)},
            device_id_type=MESH,
        )

    def text_copy(j):
        to = lax.rem(seq + j, SEQ)
        return pltpu.make_async_remote_copy(
            src_ref=send.at[to],
            dst_ref=got.at[seq],
            send_sem=txt_send.at[j],
            recv_sem=txt_recv.at[j],
            device_id={"seq": to, "head": head},
            device_id_type=MESH,
        )

    def start_of(copy):
        def body(j, carry):
            copy(j).start()
            return carry
        return body

    def wait_of(copy):
        def body(j, carry):
            copy(j).wait()
            return carry
        return body

    lax.fori_loop(1, HEAD, start_of(square_copy), 0)
    halo_start(0, 0)

    frames = [shapes[s, 0] for s in range(SAMPLES)]
    ends = []
    running = jnp.int32(0)
    for s in range(SAMPLES):
        running = running + frames[s]
        ends.append(running)

    def video_of(frame):
        sample = jnp.int32(0)
        first = jnp.int32(0)
        for s in range(SAMPLES - 1):
            past = frame >= ends[s]
            sample = sample + jnp.where(past, 1, 0)
            first = first + jnp.where(past, frames[s], 0)
        return sample, first

    def pack(e, carry):
        for slot in range(2):
            sample, _ = video_of(2 * e + slot)
            panel = owner[sample]
            for kv in range(2):
                send[e, slot, kv] = text[kv, panel]
        return carry

    lax.fori_loop(0, SEQ, pack, 0)

    places = []
    for offset in (-1, 0, 1, 2):
        frame = lax.rem(2 * seq + offset + 2 * SEQ, 2 * SEQ)
        sample, first = video_of(frame)
        places.append((jnp.clip(frame - first, 0, TIMES - 1), shapes[sample, 2] > 16))

    for i in range(8):
        at, land = i % 4, places[1 + i // 4][1]
        for step in range(3):
            for other in range(4):
                wide_slot = step * 9 + (other // 2 - at // 2 + 1) * 3 + (other % 2 - at % 2 + 1)
                listed = windows[i, wide_slot]
                if abs(other - at) <= 1:
                    listed_tall = windows[i, step * 9 + (other - at + 1) * 3 + 1]
                else:
                    listed_tall = jnp.int32(-1)
                chosen = jnp.where(land, listed, listed_tall)
                bias[i * 12 + step * 4 + other] = jnp.where(chosen >= 0, jnp.float32(0.0), jnp.float32(MASKED))

    lax.fori_loop(1, HEAD, wait_of(square_copy), 0)
    whole = squares[...]
    for j in range(HEAD - 1):
        whole = whole + peer_squares[j]
    totals[...] = whole[8:16]

    def total_copy(direction):
        return pltpu.make_async_remote_copy(
            src_ref=totals,
            dst_ref=halo_totals.at[direction],
            send_sem=tot_send.at[direction],
            recv_sem=tot_recv.at[direction],
            device_id={"seq": (right, left)[direction], "head": head},
            device_id_type=MESH,
        )

    inverse[...] = lax.rsqrt(whole / D + EPSILON)
    for direction in range(2):
        total_copy(direction).start()
    own_text = pltpu.make_async_copy(send.at[seq], got.at[seq], own_sem)
    own_text.start()
    lax.fori_loop(1, SEQ, start_of(text_copy), 0)
    lax.fori_loop(1, HEADS, halo_start, 0)

    def tables(place, w):
        t, land = place
        b = jnp.where(land, w // 2, w)
        c = jnp.where(land, lax.rem(w, 2), 0)
        made = []
        for n in range(3):
            rest = col_tab[n, c] + time_tab[n, pl.ds(t, 1), :]
            rows = row_tab[n, b]
            made.append(jnp.concatenate([rows[a : a + 1] + rest for a in range(8)], axis=0))
        return made

    def column(row):
        return jnp.broadcast_to(row, (TILE, HEAD_DIM)).T

    def turned(x, inv, gain, cosine, sine_a, sine_b):
        y = x.astype(jnp.float32) * inv * gain
        return (y * cosine + pltpu.roll(y, HEAD_DIM - 1, 1) * sine_a + pltpu.roll(y, 1, 1) * sine_b).astype(jnp.bfloat16)

    for frame in range(2):
        def prepare(w, carry, frame=frame):
            i = frame * 4 + w
            at = pl.ds(pl.multiple_of(i * TILE, TILE), TILE)
            tabs = tables(places[1 + frame], w)
            inv_q = column(inverse[pl.ds(i, 1), :])
            inv_k = column(inverse[pl.ds(8 + i, 1), :])
            for h in range(HEADS):
                qx[h, at, :] = turned(qx[h, at, :], inv_q, query_gain[h : h + 1, :], *tabs)
                kx[h, at, :] = turned(kx[h, at, :], inv_k, key_gain[h : h + 1, :], *tabs)
            return carry
        lax.fori_loop(0, 4, prepare, 0)

    for direction in range(2):
        total_copy(direction).wait()
    halo_inverse = lax.rsqrt(halo_totals[...] / D + EPSILON)
    halo_totals[...] = halo_inverse
    for direction in range(2):
        def prepare_halo(w, carry, direction=direction):
            cosine, sine_a, sine_b = tables(places[3 * direction], w)
            i = direction * 4 + w
            cos_h[i] = cosine
            sina_h[i] = sine_a
            sinb_h[i] = sine_b
            inv_h[i] = column(halo_totals[direction, pl.ds((1 - direction) * 4 + w, 1), :])
            return carry
        lax.fori_loop(0, 4, prepare_halo, 0)

    lax.fori_loop(1, SEQ, wait_of(text_copy), 0)
    own_text.wait()

    sharp = np.float32(HEAD_DIM ** -0.5 * np.log2(np.e))
    last_dims = (((1,), (1,)), ((), ()))

    def out_copy(h, frame):
        return pltpu.make_async_copy(
            outs.at[h, pl.ds(frame * FRAME, FRAME), :],
            out_hbm.at[pl.ds(frame * FRAME, FRAME), pl.ds(pl.multiple_of(h * HEAD_DIM, HEAD_DIM), HEAD_DIM)],
            out_sem.at[h, frame],
        )

    def attend(h, carry):
        for kv in range(2):
            for direction in range(2):
                halo_copy(h, kv, direction).wait()
        gain = key_gain[pl.ds(h, 1), :]
        for direction in range(2):
            for w in range(4):
                i = direction * 4 + w
                at = pl.ds(w * TILE, TILE)
                hk[direction, h, at, :] = turned(hk[direction, h, at, :], inv_h[i], gain, cos_h[i], sina_h[i], sinb_h[i])
        lanes = pl.ds(pl.multiple_of(h * HEAD_DIM, HEAD_DIM), HEAD_DIM)
        for frame in range(2):
            text_k = got[:, frame, 0, :, lanes].reshape(TXT, HEAD_DIM)
            text_v = got[:, frame, 1, :, lanes].reshape(TXT, HEAD_DIM)
            if frame == 0:
                keys = (hk[0, h], kx[h], text_k)
                values = (hv[0, h], vx[h], text_v)
            else:
                keys = (kx[h], hk[1, h], text_k)
                values = (vx[h], hv[1, h], text_v)
            for half in range(2):
                first = frame * FRAME + half * 256
                q = qx[h, pl.ds(first, 256), :]
                scores = jnp.concatenate(
                    [lax.dot_general(q, k, last_dims, preferred_element_type=jnp.float32) for k in keys], axis=1
                )
                masked = []
                for part in range(2):
                    i = frame * 4 + half * 2 + part
                    band = scores[part * TILE : (part + 1) * TILE]
                    pieces = [band[:, j * TILE : (j + 1) * TILE] + bias[i * 12 + j] for j in range(12)]
                    masked.append(jnp.concatenate(pieces + [band[:, 12 * TILE :]], axis=1))
                scores = jnp.concatenate(masked, axis=0)
                largest = jnp.max(scores, axis=1, keepdims=True)
                weights = jnp.exp2((scores - largest) * sharp)
                total = jnp.sum(weights, axis=1, keepdims=True)
                weights = weights.astype(jnp.bfloat16)
                mixed = jnp.zeros((256, HEAD_DIM), jnp.float32)
                begin = 0
                for v in values:
                    mixed = mixed + jnp.dot(weights[:, begin : begin + v.shape[0]], v, preferred_element_type=jnp.float32)
                    begin += v.shape[0]
                outs[h, pl.ds(first, 256), :] = (mixed / total).astype(jnp.bfloat16)
            out_copy(h, frame).start()
        return carry

    lax.fori_loop(0, HEADS, attend, 0)

    def finish(h, carry):
        for frame in range(2):
            out_copy(h, frame).wait()
        return carry

    lax.fori_loop(0, HEADS, finish, 0)


def local(queries, keys, values, query_gain, key_gain, shapes, windows, text_keys, text_values, owner):
    time_tab, row_tab, col_tab = (jnp.asarray(t) for t in rope_tables())
    smem = pl.BlockSpec(memory_space=pltpu.SMEM)
    vmem = pl.BlockSpec(memory_space=pltpu.VMEM)
    hbm = pl.BlockSpec(memory_space=pl.ANY)
    bf16, f32 = jnp.bfloat16, jnp.float32
    dma = pltpu.SemaphoreType.DMA
    return pl.pallas_call(
        kernel,
        out_shape=jax.ShapeDtypeStruct((ROWS, HEADS * HEAD_DIM), bf16),
        in_specs=[smem] * 3 + [vmem] * 5 + [hbm] * 5,
        out_specs=hbm,
        scratch_shapes=[
            pltpu.VMEM((HEADS, ROWS, HEAD_DIM), bf16),
            pltpu.VMEM((HEADS, ROWS, HEAD_DIM), bf16),
            pltpu.VMEM((HEADS, ROWS, HEAD_DIM), bf16),
            pltpu.VMEM((2, PANELS, TXT_ROWS, HEADS * HEAD_DIM), bf16),
            pltpu.VMEM((SEQ, 2, 2, TXT_ROWS, HEADS * HEAD_DIM), bf16),
            pltpu.VMEM((SEQ, 2, 2, TXT_ROWS, HEADS * HEAD_DIM), bf16),
            pltpu.VMEM((2, HEADS, FRAME, HEAD_DIM), bf16),
            pltpu.VMEM((2, HEADS, FRAME, HEAD_DIM), bf16),
            pltpu.VMEM((16, HEAD_DIM), f32),
            pltpu.VMEM((HEAD - 1, 16, HEAD_DIM), f32),
            pltpu.VMEM((8, HEAD_DIM), f32),
            pltpu.VMEM((2, 8, HEAD_DIM), f32),
            pltpu.VMEM((16, HEAD_DIM), f32),
            pltpu.VMEM((8, TILE, HEAD_DIM), f32),
            pltpu.VMEM((8, TILE, HEAD_DIM), f32),
            pltpu.VMEM((8, TILE, HEAD_DIM), f32),
            pltpu.VMEM((8, TILE, HEAD_DIM), f32),
            pltpu.VMEM((HEADS, ROWS, HEAD_DIM), bf16),
            pltpu.SMEM((96,), f32),
            dma((3, HEADS + 1)),
            dma((2, 2, HEADS)),
            dma((2, 2, HEADS)),
            dma((HEAD - 1,)),
            dma((HEAD - 1,)),
            dma((2,)),
            dma((2,)),
            dma((SEQ,)),
            dma((SEQ,)),
            dma,
            dma((HEADS, 2)),
        ],
        compiler_params=pltpu.CompilerParams(
            collective_id=0, has_side_effects=True, vmem_limit_bytes=56 * 1024 * 1024
        ),
        cost_estimate=pl.CostEstimate(flops=5 * 10**9, bytes_accessed=12 * 10**6, transcendentals=10**7),
        name="window_prompt_attention",
    )(
        shapes, windows, owner,
        query_gain.reshape(HEADS, HEAD_DIM), key_gain.reshape(HEADS, HEAD_DIM),
        time_tab, row_tab, col_tab,
        queries, keys, values, text_keys, text_values,
    )


def solution(mesh):
    placed = (
        P("seq", "head"),
        P("seq", "head"),
        P("seq", "head"),
        P("head"),
        P("head"),
        P(),
        P("seq", None),
        P(None, "seq", "head"),
        P(None, "seq", "head"),
        P(),
    )
    return jax.shard_map(
        local, mesh=mesh, in_specs=placed, out_specs=P("seq", "head"), check_vma=False
    )
```
